32 devices in a mesh: grp: 2 (over y), col: 4 (over x, core), row: 4 (over z).
Axes of the slice: x: 2, y: 2, z: 4, core: 2. Of those that a mesh axis runs over, the one named last changes fastest.
Arguments:
- tokens: bfloat16 [1024, 7168], P(('grp', 'col'), 'row'), parts along dimension 0, may hold values from -6 to 6
- expert_ids: int32 [1024, 8], P(('grp', 'col')), parts along dimension 0, may hold values from 0 to 15, all different within a row; in each aligned block of 128 rows (0 to 127, 128 to 255, ...) at most 80 rows name the same one
- weight_index: int32 [1024, 8], P(('grp', 'col')), parts along dimension 0, may hold values from 0 to 63
- combine_table: float32 [64], replicated, may hold values from 0.1 to 1
- gate_weight: bfloat16 [16, 7168, 2048], P('col', None, 'row'), may hold values from -0.0625 to 0.0625
- up_weight: bfloat16 [16, 7168, 2048], P('col', None, 'row'), may hold values from -0.0625 to 0.0625
- down_weight: bfloat16 [16, 2048, 7168], P('col', None, 'row'), may hold values from -0.125 to 0.125
Outputs:
- layer_output: bfloat16 [1024, 7168], P(('grp', 'col'), 'row'), parts along dimension 0
The draws below stay inside these ranges and needn't reach their ends.
There are 2 independent parts, one for each index of `grp`. The reference program is written for one: setup_inputs(seed, part) draws one part's arguments, and reference() takes and returns one part's arrays. A program takes and returns all parts, laid end to end along the dimension named above; an argument that names none is the same for every part. Nothing has to cross between parts.
Inputs may be any that keep to these rules, and one draw needn't show every extreme that they name: `expert_ids`: each row names 8 different experts, and every expert is named somewhere. Within the 128 rows of one index of col (aligned blocks), no expert is named by more than 80 rows.
All inputs are finite; a program needn't handle non-finite values.
Results may differ from the reference program's by a relative error of at most 0.0057.
Values may be sent and summed in bfloat16 or wider, within the bound.
No kernel may reach another device: no remote copies, remote signals or barrier semaphores. Data moves between devices by JAX's collectives and lax.ppermute only.
A program may use at most 192 MiB of HBM per device.

```python
import math
from functools import partial
import jax
import jax.numpy as jnp
import numpy as np
from jax import lax

D = 7168
FF = 2048
TOP = 8
EXPERTS = 16
TABLE = 64
TOK_DEV = 128
CAP = 80
TOKENS = 512


def with_ends(result, key, least, high):
    place = [jax.random.randint(jax.random.fold_in(key, axis), (), 0, length) for axis, length in enumerate(result.shape)]
    longest = result.shape.index(max(result.shape))
    neighbour = place[:longest] + [(place[longest] + 1) % result.shape[longest]] + place[longest + 1:]
    return result.at[tuple(place)].set(least).at[tuple(neighbour)].set(high)


def block_levels(key, dims, pieces, smallest, top_value):
    gain = 1.0
    for position, blocks in pieces:
        steps = jax.random.uniform(jax.random.fold_in(jax.random.fold_in(key, 6), position), (blocks,), jnp.float32, smallest / len(pieces), top_value / len(pieces))
        gain = gain * jnp.repeat(jnp.exp(steps), dims[position] // blocks).reshape((-1,) + (1,) * (len(dims) - 1 - position))
    return gain


def routed_block(stream_key, own, number, rows, amount, top, most, slope):
    order = jax.random.permutation(stream_key, amount)
    packed, common = load_shares(amount, rows * top, most, slope, True), load_shares(amount, rows * top, most, slope, False)
    places = jnp.arange(amount)

    def named(sizes, turn):
        used = int((sizes > 0).sum())
        fixed = max(1, used // 4)
        moved = fixed + (places - fixed + turn * (used - fixed)) % max(1, amount - fixed)
        return jnp.zeros((amount,), jnp.int32).at[order[jnp.where(places < fixed, places, moved)]].set(jnp.asarray(sizes, jnp.int32))

    sizes = jnp.where(number % 4 == 0, named(packed, number // 4), named(common, number - number // 4 - 1))
    mixed = jax.random.permutation(jax.random.fold_in(own, 3), amount)
    giver, receiver = mixed[0:amount // 2 * 2:2], mixed[1:amount // 2 * 2:2]
    margin = jnp.minimum(sizes[giver] - 1, most - sizes[receiver]) // 2
    margin = jnp.where((giver == order[0]) | (receiver == order[0]) | (sizes[receiver] == 0), 0, jnp.maximum(margin, 0))
    moved = jax.random.randint(jax.random.fold_in(own, 4), (amount // 2,), 0, 1 << 20) % (margin + 1)
    sizes = sizes.at[giver].add(-moved).at[receiver].add(moved)
    members = jnp.searchsorted(jnp.cumsum(sizes), jnp.arange(rows * top), side="right").astype(jnp.int32)
    grid = members.reshape(top, rows).T
    grid = grid[jax.random.permutation(jax.random.fold_in(own, 1), rows)]
    turn = jax.random.randint(jax.random.fold_in(own, 2), (rows, 1), 0, top)
    return jnp.take_along_axis(grid, (jnp.arange(top)[None, :] + turn) % top, axis=1)


def load_shares(amount, total, limit, skew, full):
    portions = [(1 << 20) // math.isqrt(rank ** skew) + 1 for rank in range(1, amount + 1)]
    largest = limit if full else min(limit, max(-(-total // amount), total * portions[0] // sum(portions)))
    least = 1 if total - largest >= amount - 1 else 0
    counts, surplus = [largest] + [least] * (amount - 1), total - largest - least * (amount - 1)
    while surplus > 0:
        free = [i for i in range(1, amount) if counts[i] < largest] or [i for i in range(1, amount) if counts[i] < limit]
        whole, remaining = sum([portions[i] for i in free]), surplus
        for i in free:
            extra = min(limit - counts[i], max(1, remaining * portions[i] // whole), surplus)
            counts[i] = counts[i] + extra
            surplus = surplus - extra
    return np.array(counts)


def noise(key, dims, deviation, most, cuts=(), kind=jnp.bfloat16):
    array = jax.random.normal(key, dims, jnp.float32) * deviation
    if len(cuts) > 0:
        array = block_levels(key, dims, cuts, -0.22, 0.18) * array
    return jnp.clip(array, min=-most, max=most).astype(kind)


def setup_inputs(seed: int = 0, part: int = 0) -> dict:
    keys = jax.random.split(jax.random.key(seed), 8)
    part_splits = jax.random.split(jax.random.fold_in(keys[7], part), 8)
    tokens = noise(part_splits[0], (TOKENS, D), 1.0, 6.0, ((0, 4), (1, 4)))
    expert_ids_keys = jax.random.split(jax.random.fold_in(part_splits[1], 1), TOKENS // TOK_DEV)
    expert_ids_turns = jax.random.permutation(jax.random.fold_in(part_splits[1], 3), TOKENS // TOK_DEV)
    expert_ids = jax.vmap(lambda own, number: routed_block(jax.random.fold_in(part_splits[1], 2), own, number, TOK_DEV, EXPERTS, TOP, CAP, 2))(expert_ids_keys, expert_ids_turns).reshape((TOKENS, TOP))
    weight_index = with_ends(jax.random.randint(part_splits[2], (TOKENS, TOP), 0, TABLE), jax.random.fold_in(part_splits[2], 1), 0, TABLE - 1).astype(jnp.int32)
    combine_table = jnp.clip(jnp.exp(jax.random.uniform(keys[3], (TABLE,), jnp.float32, math.log(0.1), math.log(1.0))), 0.1, 1.0)
    gate_weight = noise(keys[4], (EXPERTS, D, FF), D ** -0.5, 0.0625, ((0, 4), (2, 4)))
    up_weight = noise(keys[5], (EXPERTS, D, FF), D ** -0.5, 0.0625, ((0, 4), (2, 4)))
    down_weight = noise(keys[6], (EXPERTS, FF, D), FF ** -0.5, 0.125, ((0, 4), (2, 4)))
    return dict(tokens=tokens, expert_ids=expert_ids, weight_index=weight_index, combine_table=combine_table, gate_weight=gate_weight, up_weight=up_weight, down_weight=down_weight)


route_scale = 2.827


def slot_table(picked_ids, experts, capacity):
    count, picks = picked_ids.shape
    flat_ids = picked_ids.reshape(-1).astype(jnp.int32)
    one_hot = (flat_ids[:, None] == jnp.arange(experts, dtype=jnp.int32)[None, :]).astype(jnp.int32)
    ranking = jnp.sum((jnp.cumsum(one_hot, axis=0) - 1) * one_hot, axis=1).astype(jnp.int32)
    placing = (flat_ids * capacity + ranking).astype(jnp.int32)
    entries = (jnp.arange(count * picks, dtype=jnp.int32) // picks).astype(jnp.int32)
    holder = jnp.full((experts * capacity,), -1, jnp.int32).at[placing].set(entries)
    return holder, placing


def combine_weights(weight_index, combine_table):
    table_size = combine_table.shape[0]
    match = weight_index[..., None] == jnp.arange(table_size, dtype=jnp.int32)
    table_values = jnp.sum(jnp.where(match, combine_table.astype(jnp.float32), jnp.float32(0.0)), axis=-1)
    return route_scale * table_values / jnp.sum(table_values, axis=-1, keepdims=True)


def reference(tokens, expert_ids, weight_index, combine_table, gate_weight, up_weight, down_weight):
    groups = TOKENS // TOK_DEV
    block_ids = expert_ids.reshape(groups, TOK_DEV, TOP)
    holder, placing = jax.vmap(partial(slot_table, experts=EXPERTS, capacity=CAP))(block_ids)
    offsets = (jnp.arange(groups, dtype=jnp.int32) * TOK_DEV)[:, None]
    global_holder = jnp.where(holder >= 0, holder + offsets, -1).astype(jnp.int32)
    slot_lists = global_holder.reshape(groups, EXPERTS, CAP).transpose(1, 0, 2).reshape(EXPERTS, groups * CAP)

    def expert(operands):
        slot_index, gate_mat, up_mat, down_mat = operands
        is_valid = slot_index >= 0
        routed_rows = jnp.take(tokens, jnp.maximum(slot_index, 0), axis=0)
        routed_rows = jnp.where(is_valid[:, None], routed_rows, jnp.zeros((), tokens.dtype))
        gate_part = jnp.dot(routed_rows, gate_mat, preferred_element_type=jnp.float32)
        up_part = jnp.dot(routed_rows, up_mat, preferred_element_type=jnp.float32)
        hidden = (jax.nn.silu(gate_part) * up_part).astype(jnp.bfloat16)
        return jnp.dot(hidden, down_mat, preferred_element_type=jnp.float32).astype(jnp.bfloat16)

    expert_out = lax.map(expert, (slot_lists, gate_weight, up_weight, down_weight))
    group_base = (jnp.arange(groups, dtype=jnp.int32) * CAP)[:, None]
    found = ((placing // CAP) * (groups * CAP) + group_base + placing % CAP).astype(jnp.int32)
    gathered = jnp.take(expert_out.reshape(EXPERTS * groups * CAP, D), found.reshape(-1), axis=0)
    gathered = gathered.reshape(TOKENS, TOP, D).astype(jnp.float32)
    weights = combine_weights(weight_index, combine_table)
    return jnp.sum(weights[..., None] * gathered, axis=1).astype(jnp.bfloat16)
```

```python
import functools

import jax
import jax.numpy as jnp
from jax import lax
from jax.experimental import pallas as pl
from jax.experimental.pallas import tpu as pltpu
from jax.sharding import PartitionSpec as P

CAP = 80
route_scale = 2.827
BF = jnp.bfloat16
F32 = jnp.float32
VMEM_LIMIT = 60 * 1024 * 1024


def tile_of(size, most):
    best = 128
    for width in range(128, most + 1, 128):
        if size % width == 0:
            best = width
    return best if size % best == 0 else size


def combine_weights(weight_index, combine_table):
    table_size = combine_table.shape[0]
    match = weight_index[..., None] == jnp.arange(table_size, dtype=jnp.int32)
    table_values = jnp.sum(jnp.where(match, combine_table, jnp.float32(0.0)), axis=-1)
    return route_scale * table_values / jnp.sum(table_values, axis=-1, keepdims=True)


def expert_weights(expert_ids, weight_index, combine_table, experts):
    weights = combine_weights(weight_index, combine_table)
    match = expert_ids[None] == jnp.arange(experts, dtype=jnp.int32)[:, None, None]
    return jnp.sum(jnp.where(match, weights[None], jnp.float32(0.0)), axis=-1)


def slots_of(weights):
    count = weights.shape[-1]
    named = weights > 0
    row = lax.broadcasted_iota(jnp.int32, (count, count), 0)
    column = lax.broadcasted_iota(jnp.int32, (count, count), 1)
    before = (row < column).astype(BF)
    rank = jnp.einsum("bet,tu->beu", named.astype(BF), before, preferred_element_type=F32)
    return jnp.where(named, rank.astype(jnp.int32), -1)


class Links:
    def __init__(self):
        self.cols = lax.axis_size("col")
        self.rows = lax.axis_size("row")
        self.cores = 2 if self.cols % 2 == 0 else 1
        self.chips = self.cols // self.cores
        self.z = lax.axis_index("row")

    def send(self, value, target, sends=lambda z: True):
        pairs = []
        for col in range(self.cols):
            for z in range(self.rows):
                if sends(z):
                    to_col, to_z = target(col, z)
                    pairs.append((col * self.rows + z, to_col * self.rows + to_z))
        return lax.ppermute(value, ("col", "row"), pairs)

    def swap_core(self, value, holds=lambda z: True):
        return self.send(value, lambda col, z: (col ^ 1, z), holds)

    def shift_chip(self, value, distance, holds=lambda z: True):
        step = distance * self.cores
        return self.send(value, lambda col, z: ((col + step) % self.cols, z), holds)

    def row_plan(self):
        rows = self.rows
        if rows != 4:
            return [(lambda z, s=s: True, lambda z, s=s: (z - s) % rows) for s in range(rows)]
        return [
            (lambda z: True, lambda z: z),
            (lambda z: z > 0, lambda z: z - 1),
            (lambda z: z < 3, lambda z: z + 1),
            (lambda z: True, lambda z: (z + 2) % 4),
            (lambda z: z % 3 == 0, lambda z: 3 - z),
        ]

    def gather_row(self, value):
        rows = self.rows
        if rows != 4:
            return [value] + [
                self.send(value, lambda col, z, s=s: (col, (z + s) % rows)) for s in range(1, rows)
            ]
        right = self.send(value, lambda col, z: (col, z + 1), lambda z: z < 3)
        left = self.send(value, lambda col, z: (col, z - 1), lambda z: z > 0)
        far = self.send(value, lambda col, z: (col, (z + 2) % 4))
        end = self.send(far, lambda col, z: (col, 3 if z == 2 else 0), lambda z: z in (1, 2))
        return [value, right, left, far, end]

    def row_tables(self):
        plan = self.row_plan()
        picks, origins, valid, source = [], [], [], []
        for z in range(self.rows):
            held = [(r, of(z)) for r, (has, of) in enumerate(plan) if has(z)]
            picks.append([r for r, _ in held])
            origins.append([o for _, o in held])
            valid.append([int(has(z)) for has, _ in plan])
            source.append([of(z) if has(z) else 0 for has, of in plan])
        take = lambda table: jnp.asarray(table, jnp.int32)[self.z]
        return take(picks), take(origins), take(valid), take(source)


def dispatch(pieces, slots, picks, origins, rows):
    local, count = slots.shape
    width = pieces[0].shape[1]
    number = len(pieces)

    def body(picks_ref, origins_ref, slots_ref, *refs):
        piece_refs, out_ref, hot_ref = refs[:number], refs[number], refs[number + 1]
        step = pl.program_id(0)

        @pl.when(step == 0)
        def _():
            place = lax.broadcasted_iota(jnp.int32, (CAP, count), 0)
            for e in range(local):
                hot_ref[pl.ds(e * CAP, CAP), :] = jnp.where(place == slots_ref[e : e + 1, :], 1.0, 0.0).astype(BF)

        for r in range(number):

            @pl.when(picks_ref[step] == r)
            def _(r=r):
                got = jnp.dot(hot_ref[...], piece_refs[r][...], preferred_element_type=F32).astype(BF)
                for e in range(local):
                    out_ref[e] = got[e * CAP : (e + 1) * CAP]

    whole = pl.BlockSpec((count, width), lambda i, p, o: (0, 0), pipeline_mode=pl.Buffered(1))
    return pl.pallas_call(
        body,
        out_shape=jax.ShapeDtypeStruct((local, CAP, width * rows), BF),
        grid_spec=pltpu.PrefetchScalarGridSpec(
            num_scalar_prefetch=2,
            grid=(rows,),
            in_specs=[pl.BlockSpec((local, count), lambda i, p, o: (0, 0))] + [whole] * number,
            out_specs=pl.BlockSpec((local, CAP, width), lambda i, p, o: (0, 0, o[i])),
            scratch_shapes=[pltpu.VMEM((local * CAP, count), BF)],
        ),
        compiler_params=pltpu.CompilerParams(
            dimension_semantics=("arbitrary",), vmem_limit_bytes=VMEM_LIMIT
        ),
        cost_estimate=pl.CostEstimate(
            flops=4 * local * CAP * count * width * rows,
            bytes_accessed=2 * width * rows * (count + local * CAP),
            transcendentals=0,
        ),
        name="dispatch",
    )(picks, origins, slots, *pieces)


def gate_up(blocks, gate_weight, up_weight, e):
    number = len(blocks)
    model, units = gate_weight.shape[1:]
    depth = tile_of(model, 1024)
    steps = model // depth
    rows = number * CAP

    def body(*refs):
        block_refs = refs[:number]
        gate_ref, up_ref, out_ref, gate_sum, up_sum = refs[number:]
        step = pl.program_id(0)
        source = jnp.concatenate([ref[...] for ref in block_refs], axis=0)
        gate = jnp.dot(source, gate_ref[...], preferred_element_type=F32)
        up = jnp.dot(source, up_ref[...], preferred_element_type=F32)

        @pl.when(step == 0)
        def _():
            gate_sum[...] = gate
            up_sum[...] = up

        @pl.when(step > 0)
        def _():
            gate_sum[...] += gate
            up_sum[...] += up

        @pl.when(step == steps - 1)
        def _():
            value = gate_sum[...]
            out_ref[...] = (value / (1.0 + jnp.exp(-value)) * up_sum[...]).astype(BF)

    weight = pl.BlockSpec((None, depth, units), lambda i: (e, i, 0))
    return pl.pallas_call(
        body,
        out_shape=jax.ShapeDtypeStruct((rows, units), BF),
        grid=(steps,),
        in_specs=[pl.BlockSpec((None, CAP, depth), lambda i: (e, 0, i))] * number + [weight, weight],
        out_specs=pl.BlockSpec((rows, units), lambda i: (0, 0)),
        scratch_shapes=[pltpu.VMEM((rows, units), F32)] * 2,
        compiler_params=pltpu.CompilerParams(
            dimension_semantics=("arbitrary",), vmem_limit_bytes=VMEM_LIMIT
        ),
        cost_estimate=pl.CostEstimate(
            flops=4 * rows * model * units,
            bytes_accessed=2 * model * (rows + 2 * units),
            transcendentals=rows * units,
        ),
        name="gate_up",
    )(*blocks, gate_weight, up_weight)


def down(hidden, valid, source, down_weight, e):
    number = len(hidden)
    rows, units = hidden[0].shape
    inner, width = down_weight.shape[1:]
    tile = tile_of(width, 256)

    def body(valid_ref, source_ref, *refs):
        hidden_refs, weight_ref, out_ref, joined = refs[:number], refs[number], refs[number + 1], refs[number + 2]

        @pl.when(pl.program_id(0) == 0)
        def _():
            for r in range(number):

                @pl.when(valid_ref[r] == 1)
                def _(r=r):
                    start = pl.multiple_of(source_ref[r] * units, units)
                    joined[:, pl.ds(start, units)] = hidden_refs[r][...]

        out_ref[...] = jnp.dot(joined[...], weight_ref[...], preferred_element_type=F32).astype(BF)

    whole = pl.BlockSpec((rows, units), lambda i, v, s: (0, 0), pipeline_mode=pl.Buffered(1))
    return pl.pallas_call(
        body,
        out_shape=jax.ShapeDtypeStruct((rows, width), BF),
        grid_spec=pltpu.PrefetchScalarGridSpec(
            num_scalar_prefetch=2,
            grid=(width // tile,),
            in_specs=[whole] * number + [pl.BlockSpec((None, inner, tile), lambda i, v, s: (e, 0, i))],
            out_specs=pl.BlockSpec((rows, tile), lambda i, v, s: (0, i)),
            scratch_shapes=[pltpu.VMEM((rows, inner), BF)],
        ),
        compiler_params=pltpu.CompilerParams(
            dimension_semantics=("arbitrary",), vmem_limit_bytes=VMEM_LIMIT
        ),
        cost_estimate=pl.CostEstimate(
            flops=2 * rows * inner * width,
            bytes_accessed=2 * (rows * inner + inner * width + rows * width),
            transcendentals=0,
        ),
        name="down",
    )(valid, source, *hidden, down_weight)


def combine(outs, block, slots, weights, extra, dtype):
    local, count = slots.shape
    width = outs[0].shape[1]
    extras = [] if extra is None else [extra]

    def body(slots_ref, weights_ref, *refs):
        out_refs, result = refs[:local], refs[-1]
        place = lax.broadcasted_iota(jnp.int32, (CAP, count), 0)
        share = jnp.concatenate(
            [jnp.where(place == slots_ref[e : e + 1, :], weights_ref[e : e + 1, :], 0.0) for e in range(local)], axis=0
        )
        coarse = share.astype(BF)
        fine = (share - coarse.astype(F32)).astype(BF)
        values = jnp.concatenate([ref[...] for ref in out_refs], axis=0)
        turn = (((0,), (0,)), ((), ()))
        total = lax.dot_general(coarse, values, turn, preferred_element_type=F32)
        total += lax.dot_general(fine, values, turn, preferred_element_type=F32)
        if extras:
            total += refs[local][...].astype(F32)
        result[...] = total.astype(dtype)

    small = pl.BlockSpec((local, count), lambda i: (0, 0))
    full = pl.BlockSpec((count, width), lambda i: (0, 0))
    return pl.pallas_call(
        body,
        out_shape=jax.ShapeDtypeStruct((count, width), dtype),
        grid=(1,),
        in_specs=[small, small] + [pl.BlockSpec((CAP, width), lambda i: (block, 0))] * local + [full] * len(extras),
        out_specs=full,
        compiler_params=pltpu.CompilerParams(
            dimension_semantics=("arbitrary",), vmem_limit_bytes=VMEM_LIMIT
        ),
        cost_estimate=pl.CostEstimate(
            flops=4 * local * CAP * count * width,
            bytes_accessed=2 * width * (local * CAP + 2 * count),
            transcendentals=0,
        ),
        name="combine",
    )(slots, weights, *outs, *extras)


def shards(tokens, expert_ids, weight_index, combine_table, gate_weight, up_weight, down_weight):
    links = Links()
    cores, chips, rows = links.cores, links.chips, links.rows
    local = gate_weight.shape[0]
    experts = local * links.cols
    picks, origins, valid, source = links.row_tables()
    holds = [has for has, _ in links.row_plan()]

    mine = expert_weights(expert_ids, weight_index, combine_table, experts)
    pair = [mine] + ([links.swap_core(mine)] if cores == 2 else [])
    spread = []
    for distance in range(chips):
        for value in pair:
            spread.append(links.shift_chip(value, distance) if distance else value)
    spread = jnp.stack(spread)
    weights = lax.dynamic_slice_in_dim(spread, lax.axis_index("col") * local, local, axis=1)
    slots = slots_of(weights)

    held = links.gather_row(tokens)
    pieces = []
    for distance in range(chips):
        own = [links.shift_chip(v, distance, h) if distance else v for v, h in zip(held, holds)]
        pieces.append(own)
        if cores == 2:
            pieces.append([links.swap_core(v, h) for v, h in zip(own, holds)])
    blocks = [dispatch(piece, slots[i], picks, origins, rows) for i, piece in enumerate(pieces)]

    outs = []
    for e in range(local):
        hidden = links.gather_row(gate_up(blocks, gate_weight, up_weight, e))
        outs.append(down(hidden, valid, source, down_weight, e))

    total = None
    for distance in range(chips - 1, -1, -1):
        index = distance * cores
        extra = None
        if cores == 2:
            extra = links.swap_core(combine(outs, index + 1, slots[index + 1], weights[index + 1], None, BF))
        kept = combine(outs, index, slots[index], weights[index], extra, BF if distance else F32)
        got = links.shift_chip(kept, chips - distance).astype(F32) if distance else kept
        total = got if total is None else total + got
    return total.astype(BF)


def solution(mesh):
    in_specs = (
        P(("grp", "col"), "row"),
        P(("grp", "col"), None),
        P(("grp", "col"), None),
        P(),
        P("col", None, "row"),
        P("col", None, "row"),
        P("col", None, "row"),
    )
    out_specs = P(("grp", "col"), "row")
    return jax.shard_map(shards, mesh=mesh, in_specs=in_specs, out_specs=out_specs, check_vma=False)
```

```python
import jax
import jax.numpy as jnp
from jax import lax
from jax.experimental import pallas as pl
from jax.experimental.pallas import tpu as pltpu
from jax.sharding import PartitionSpec as P

CAP = 80
route_scale = 2.827
BF = jnp.bfloat16
F32 = jnp.float32


def tile_of(size, most):
    best = 128
    for width in range(128, most + 1, 128):
        if size % width == 0:
            best = width
    return best if size % best == 0 else size


def combine_weights(weight_index, combine_table):
    table_size = combine_table.shape[0]
    match = weight_index[..., None] == jnp.arange(table_size, dtype=jnp.int32)
    table_values = jnp.sum(jnp.where(match, combine_table, jnp.float32(0.0)), axis=-1)
    return route_scale * table_values / jnp.sum(table_values, axis=-1, keepdims=True)


def expert_weights(expert_ids, weight_index, combine_table, experts):
    weights = combine_weights(weight_index, combine_table)
    match = expert_ids[None] == jnp.arange(experts, dtype=jnp.int32)[:, None, None]
    return jnp.sum(jnp.where(match, weights[None], jnp.float32(0.0)), axis=-1)


def slots_of(weights):
    count = weights.shape[-1]
    named = weights > 0
    row = lax.broadcasted_iota(jnp.int32, (count, count), 0)
    column = lax.broadcasted_iota(jnp.int32, (count, count), 1)
    before = (row < column).astype(BF)
    rank = jnp.einsum("bet,tu->beu", named.astype(BF), before, preferred_element_type=F32)
    return jnp.where(named, rank.astype(jnp.int32), -1)


class Links:
    def __init__(self):
        self.cols = lax.axis_size("col")
        self.rows = lax.axis_size("row")
        self.cores = 2 if self.cols % 2 == 0 else 1
        self.chips = self.cols // self.cores
        self.z = lax.axis_index("row")

    def send(self, value, target, sends=lambda z: True):
        pairs = []
        for col in range(self.cols):
            for z in range(self.rows):
                if sends(z):
                    to_col, to_z = target(col, z)
                    pairs.append((col * self.rows + z, to_col * self.rows + to_z))
        return lax.ppermute(value, ("col", "row"), pairs)

    def shift(self, value, distance, core, holds=lambda z: True):
        step = distance * self.cores
        return self.send(value, lambda col, z: (((col ^ core) + step) % self.cols, z), holds)

    def row_plan(self):
        rows = self.rows
        if rows != 4:
            return [(lambda z, s=s: True, lambda z, s=s: (z - s) % rows) for s in range(rows)]
        return [
            (lambda z: True, lambda z: z),
            (lambda z: z > 0, lambda z: z - 1),
            (lambda z: z < 3, lambda z: z + 1),
            (lambda z: True, lambda z: (z + 2) % 4),
            (lambda z: z % 3 == 0, lambda z: 3 - z),
        ]

    def gather_row(self, value):
        rows = self.rows
        if rows != 4:
            return [value] + [
                self.send(value, lambda col, z, s=s: (col, (z + s) % rows)) for s in range(1, rows)
            ]
        right = self.send(value, lambda col, z: (col, z + 1), lambda z: z < 3)
        left = self.send(value, lambda col, z: (col, z - 1), lambda z: z > 0)
        far = self.send(value, lambda col, z: (col, (z + 2) % 4))
        end = self.send(far, lambda col, z: (col, 3 if z == 2 else 0), lambda z: z in (1, 2))
        return [value, right, left, far, end]

    def row_tables(self):
        plan = self.row_plan()
        picks, origins = [], []
        for z in range(self.rows):
            held = [(r, of(z)) for r, (has, of) in enumerate(plan) if has(z)]
            picks.append([r for r, _ in held])
            origins.append([o for _, o in held])
        take = lambda table: jnp.asarray(table, jnp.int32)[self.z]
        return take(picks), take(origins)


def gate_up(pieces, slots, picks, origins, gate_weight, up_weight, e):
    number, raw = len(pieces), len(pieces[0])
    rows = picks.shape[0]
    count, width = pieces[0][0].shape
    model, units = gate_weight.shape[1:]
    tile = tile_of(units, 256)
    chunks = units // tile
    depth = rows if rows <= 4 else 2
    total = number * CAP

    def body(picks_ref, origins_ref, slots_ref, *refs):
        piece_refs = refs[: number * raw]
        gate_ref, up_ref, out_ref, arrived, source, gate_in, up_in, sem_x, sem_w = refs[number * raw :]

        def start(i):
            for r in range(raw):

                @pl.when(picks_ref[i] == r)
                def _(r=r):
                    for j in range(number):
                        pltpu.make_async_copy(
                            piece_refs[j * raw + r], arrived.at[lax.rem(i, depth), j], sem_x.at[lax.rem(i, depth), j]
                        ).start()

        def copy_of(weight_ref, into, kind, n):
            lanes = pl.ds(pl.multiple_of(n * tile, tile), tile)
            return pltpu.make_async_copy(weight_ref.at[e, :, lanes], into.at[n], sem_w.at[kind, n])

        for i in range(depth):
            start(i)
        for n in range(chunks):
            copy_of(gate_ref, gate_in, 0, n).start()
            copy_of(up_ref, up_in, 1, n).start()
        place = lax.broadcasted_iota(jnp.int32, (CAP, count), 0)
        @pl.loop(0, rows)
        def _(i):
            columns = pl.ds(pl.multiple_of(origins_ref[i] * width, 128), width)
            slot = lax.rem(i, depth)
            for j in range(number):
                pltpu.make_async_copy(piece_refs[j * raw], arrived.at[slot, j], sem_x.at[slot, j]).wait()
                hot = jnp.where(place == slots_ref[j, e : e + 1, :], 1.0, 0.0).astype(BF)
                got = jnp.dot(hot, arrived[slot, j], preferred_element_type=F32)
                source[pl.ds(j * CAP, CAP), columns] = got.astype(BF)
            if depth < rows:

                @pl.when(i + depth < rows)
                def _():
                    start(i + depth)

        @pl.loop(0, chunks)
        def _(n):
            copy_of(gate_ref, gate_in, 0, n).wait()
            gate = jnp.dot(source[...], gate_in[n], preferred_element_type=F32)
            copy_of(up_ref, up_in, 1, n).wait()
            up = jnp.dot(source[...], up_in[n], preferred_element_type=F32)
            lanes = pl.ds(pl.multiple_of(n * tile, tile), tile)
            out_ref[:, lanes] = (gate / (1.0 + jnp.exp(-gate)) * up).astype(BF)

    anywhere = pl.BlockSpec(memory_space=pl.ANY)
    scalar = pl.BlockSpec(memory_space=pltpu.SMEM)
    vector = pl.BlockSpec(memory_space=pltpu.VMEM)
    held = 2 * (depth * number * count * width + total * model + 2 * model * units + total * units)
    return pl.pallas_call(
        body,
        out_shape=jax.ShapeDtypeStruct((total, units), BF),
        in_specs=[scalar, scalar, vector] + [anywhere] * (number * raw + 2),
        out_specs=vector,
        scratch_shapes=[
            pltpu.VMEM((depth, number, count, width), BF),
            pltpu.VMEM((total, model), BF),
            pltpu.VMEM((chunks, model, tile), BF),
            pltpu.VMEM((chunks, model, tile), BF),
            pltpu.SemaphoreType.DMA((depth, number)),
            pltpu.SemaphoreType.DMA((2, chunks)),
        ],
        compiler_params=pltpu.CompilerParams(vmem_limit_bytes=min(held + 8 * 2**20, 63 * 2**20)),
        cost_estimate=pl.CostEstimate(
            flops=4 * total * model * units,
            bytes_accessed=2 * model * (number * count + 2 * units),
            transcendentals=total * units,
        ),
        name="gate_up",
    )(picks, origins, slots, *[p for piece in pieces for p in piece], gate_weight, up_weight)


def down(hidden, picks, origins, down_weight, e, earlier=None, slots=None, weights=None, cores=1):
    raw = len(hidden)
    rows = picks.shape[0]
    total, units = hidden[0].shape
    inner, width = down_weight.shape[1:]
    tile = tile_of(width, 256)
    chunks = width // tile
    last = earlier is not None
    before = len(earlier) if last else 0
    number, local, count = slots.shape if last else (0, 0, 0)

    def body(picks_ref, origins_ref, *refs):
        refs = list(refs)
        take = lambda n: [refs.pop(0) for _ in range(n)]
        hidden_refs = take(raw)
        (weight_ref,) = take(1)
        earlier_refs = take(before)
        if last:
            slots_ref, weights_ref = take(2)
        out_refs = take(number if last else 1)
        joined, weight_in, sem_h, sem_w = take(4)
        if last:
            held, coarse, fine, sem_y = take(4)
        for i in range(rows):
            columns = pl.ds(pl.multiple_of(origins_ref[i] * units, 128), units)
            for r in range(raw):

                @pl.when(picks_ref[i] == r)
                def _(r=r):
                    pltpu.make_async_copy(hidden_refs[r], joined.at[:, columns], sem_h.at[i]).start()

        def copy_of(n):
            lanes = pl.ds(pl.multiple_of(n * tile, tile), tile)
            return pltpu.make_async_copy(weight_ref.at[e, :, lanes], weight_in.at[n], sem_w.at[n])

        for n in range(chunks):
            copy_of(n).start()
        if last:
            held_copies = [pltpu.make_async_copy(ref, held.at[b], sem_y.at[b]) for b, ref in enumerate(earlier_refs)]
            for copy in held_copies:
                copy.start()
            place = lax.broadcasted_iota(jnp.int32, (CAP, count), 0)
            for j in range(number):
                share = jnp.concatenate(
                    [
                        jnp.where(place == slots_ref[j, b : b + 1, :], weights_ref[j, b : b + 1, :], 0.0)
                        for b in range(local)
                    ],
                    axis=0,
                ).T
                near = share.astype(BF)
                coarse[j] = near
                fine[j] = (share - near.astype(F32)).astype(BF)
        for i in range(rows):
            columns = pl.ds(pl.multiple_of(origins_ref[i] * units, 128), units)
            pltpu.make_async_copy(hidden_refs[0], joined.at[:, columns], sem_h.at[i]).wait()
        if last:
            for copy in held_copies:
                copy.wait()
        @pl.loop(0, chunks)
        def _(n):
            copy_of(n).wait()
            value = jnp.dot(joined[...], weight_in[n], preferred_element_type=F32).astype(BF)
            lanes = pl.ds(pl.multiple_of(n * tile, tile), tile)
            if not last:
                out_refs[0][:, lanes] = value
                return
            for j in range(number):
                block = slice(j * CAP, (j + 1) * CAP)
                values = jnp.concatenate([held[b, block, lanes] for b in range(before)] + [value[block]], axis=0)
                result = jnp.dot(coarse[j], values, preferred_element_type=F32)
                result += jnp.dot(fine[j], values, preferred_element_type=F32)
                out_refs[j][:, lanes] = result.astype(out_refs[j].dtype)

    anywhere = pl.BlockSpec(memory_space=pl.ANY)
    scalar = pl.BlockSpec(memory_space=pltpu.SMEM)
    vector = pl.BlockSpec(memory_space=pltpu.VMEM)
    scratch = [
        pltpu.VMEM((total, inner), BF),
        pltpu.VMEM((chunks, inner, tile), BF),
        pltpu.SemaphoreType.DMA((rows,)),
        pltpu.SemaphoreType.DMA((chunks,)),
    ]
    held_bytes = 2 * (total * inner + inner * width + total * width)
    if last:
        out_shape = [
            jax.ShapeDtypeStruct((count, width), BF if cores == 2 and j % 2 else F32) for j in range(number)
        ]
        scratch += [
            pltpu.VMEM((max(before, 1), total, width), BF),
            pltpu.VMEM((number, count, local * CAP), BF),
            pltpu.VMEM((number, count, local * CAP), BF),
            pltpu.SemaphoreType.DMA((max(before, 1),)),
        ]
        held_bytes += 2 * max(before, 1) * total * width + 5 * number * count * width
        extra = [slots, weights]
    else:
        out_shape = [jax.ShapeDtypeStruct((total, width), BF)]
        extra = []
    return pl.pallas_call(
        body,
        out_shape=out_shape,
        in_specs=[scalar, scalar] + [anywhere] * (raw + 1 + before) + [vector] * len(extra),
        out_specs=[vector] * len(out_shape),
        scratch_shapes=scratch,
        compiler_params=pltpu.CompilerParams(vmem_limit_bytes=min(held_bytes + 8 * 2**20, 63 * 2**20)),
        cost_estimate=pl.CostEstimate(
            flops=2 * total * inner * width,
            bytes_accessed=2 * (total * inner + inner * width + total * width * (1 + before)),
            transcendentals=0,
        ),
        name="down_combine" if last else "down",
    )(picks, origins, *hidden, down_weight, *(earlier or []), *extra)


def shards(tokens, expert_ids, weight_index, combine_table, gate_weight, up_weight, down_weight):
    links = Links()
    cores, chips = links.cores, links.chips
    local = gate_weight.shape[0]
    experts = local * links.cols
    picks, origins = links.row_tables()
    holds = [has for has, _ in links.row_plan()]

    mine = expert_weights(expert_ids, weight_index, combine_table, experts)
    spread = []
    for distance in range(chips):
        for core in range(cores):
            spread.append(links.shift(mine, distance, core) if distance or core else mine)
    spread = jnp.stack(spread)
    weights = lax.dynamic_slice_in_dim(spread, lax.axis_index("col") * local, local, axis=1)
    slots = slots_of(weights)

    held = links.gather_row(tokens)
    pieces = []
    for distance in range(chips):
        own = [links.shift(v, distance, 0, h) if distance else v for v, h in zip(held, holds)]
        pieces.append(own)
        if cores == 2:
            pieces.append([links.shift(v, 0, 1, h) for v, h in zip(own, holds)])

    outs = []
    for e in range(local):
        hidden = links.gather_row(gate_up(pieces, slots, picks, origins, gate_weight, up_weight, e))
        if e < local - 1:
            outs += down(hidden, picks, origins, down_weight, e)
        else:
            partial = down(hidden, picks, origins, down_weight, e, outs, slots, weights, cores)

    total = None
    for distance in range(chips - 1, -1, -1):
        kept = partial[distance * cores]
        if cores == 2:
            kept = kept + links.shift(partial[distance * cores + 1], 0, 1).astype(F32)
        if distance:
            kept = links.shift(kept.astype(BF), chips - distance, 0).astype(F32)
        total = kept if total is None else total + kept
    return total.astype(BF)


def solution(mesh):
    in_specs = (
        P(("grp", "col"), "row"),
        P(("grp", "col"), None),
        P(("grp", "col"), None),
        P(),
        P("col", None, "row"),
        P("col", None, "row"),
        P("col", None, "row"),
    )
    out_specs = P(("grp", "col"), "row")
    return jax.shard_map(shards, mesh=mesh, in_specs=in_specs, out_specs=out_specs, check_vma=False)
```

```python
import jax
import jax.numpy as jnp
from jax import lax
from jax.experimental import pallas as pl
from jax.experimental.pallas import tpu as pltpu
from jax.sharding import PartitionSpec as P

CAP = 80
route_scale = 2.827
BF = jnp.bfloat16
F32 = jnp.float32
GRANT = 44 * 2**20


def tile_of(size, most):
    best = 128
    for width in range(128, most + 1, 128):
        if size % width == 0:
            best = width
    return best if size % best == 0 else size


def combine_weights(weight_index, combine_table):
    table_size = combine_table.shape[0]
    match = weight_index[..., None] == jnp.arange(table_size, dtype=jnp.int32)
    table_values = jnp.sum(jnp.where(match, combine_table, jnp.float32(0.0)), axis=-1)
    return route_scale * table_values / jnp.sum(table_values, axis=-1, keepdims=True)


def expert_weights(expert_ids, weight_index, combine_table, experts):
    weights = combine_weights(weight_index, combine_table)
    match = expert_ids[None] == jnp.arange(experts, dtype=jnp.int32)[:, None, None]
    return jnp.sum(jnp.where(match, weights[None], jnp.float32(0.0)), axis=-1)


def slots_of(weights):
    count = weights.shape[-1]
    named = weights > 0
    row = lax.broadcasted_iota(jnp.int32, (count, count), 0)
    column = lax.broadcasted_iota(jnp.int32, (count, count), 1)
    before = (row < column).astype(BF)
    rank = jnp.einsum("bet,tu->beu", named.astype(BF), before, preferred_element_type=F32)
    return jnp.where(named, rank.astype(jnp.int32), -1)


class Links:
    def __init__(self):
        self.cols = lax.axis_size("col")
        self.rows = lax.axis_size("row")
        self.cores = 2 if self.cols % 2 == 0 else 1
        self.chips = self.cols // self.cores
        self.z = lax.axis_index("row")

    def send(self, value, target, sends=lambda z: True):
        pairs = []
        for col in range(self.cols):
            for z in range(self.rows):
                if sends(z):
                    to_col, to_z = target(col, z)
                    pairs.append((col * self.rows + z, to_col * self.rows + to_z))
        return lax.ppermute(value, ("col", "row"), pairs)

    def shift(self, value, distance, core, holds=lambda z: True):
        step = distance * self.cores
        return self.send(value, lambda col, z: (((col ^ core) + step) % self.cols, z), holds)

    def row_plan(self):
        rows = self.rows
        if rows != 4:
            return [(lambda z, s=s: True, lambda z, s=s: (z - s) % rows) for s in range(rows)]
        return [
            (lambda z: True, lambda z: z),
            (lambda z: z > 0, lambda z: z - 1),
            (lambda z: z < 3, lambda z: z + 1),
            (lambda z: z % 3 == 0, lambda z: 3 - z),
            (lambda z: True, lambda z: (z + 2) % 4),
        ]

    def gather_row(self, value, hops):
        rows = self.rows
        if rows != 4:
            return [value] + [self.send(value, lambda col, z, s=s: (col, (z + s) % rows)) for s in range(1, rows)]
        right = self.send(value, lambda col, z: (col, z + 1), lambda z: z < 3)
        left = self.send(value, lambda col, z: (col, z - 1), lambda z: z > 0)
        if hops:
            end = self.send(value, lambda col, z: (col, 3 - z), lambda z: z in (0, 3))
            right_far = self.send(right, lambda col, z: (col, z + 1), lambda z: z in (1, 2))
            left_far = self.send(left, lambda col, z: (col, z - 1), lambda z: z in (1, 2))
            far = jnp.where(self.z >= 2, right_far, left_far)
        else:
            far = self.send(value, lambda col, z: (col, (z + 2) % 4))
            end = self.send(far, lambda col, z: (col, 3 if z == 2 else 0), lambda z: z in (1, 2))
        return [value, right, left, end, far]

    def row_tables(self):
        plan = self.row_plan()
        picks, origins = [], []
        for z in range(self.rows):
            held = [(r, of(z)) for r, (has, of) in enumerate(plan) if has(z)]
            picks.append([r for r, _ in held])
            origins.append([o for _, o in held])
        take = lambda table: jnp.asarray(table, jnp.int32)[self.z]
        return take(picks), take(origins)


def gate_up(pieces, slots, picks, origins, gate_weight, up_weight, e, first, last, sums=None, sides=None):
    base = len(pieces[0]) - 1 if first else 0
    stop = len(pieces[0]) - (last < picks.shape[0])
    pieces = [piece[base:stop] for piece in pieces]
    number, raw = len(pieces), len(pieces[0])
    every = picks.shape[0]
    rows = last - first
    final = last == every
    count, width = pieces[0][0].shape
    _, units = gate_weight.shape[1:]
    given = [] if sums is None else list(sums)
    depth = tile_of(width, 896)
    parts = width // depth
    steps = rows * parts
    sides = sides or [(0, number)]

    def body(picks_ref, origins_ref, slots_ref, *refs):
        piece_refs = refs[: number * raw]
        refs = list(refs[number * raw :])
        take = lambda n: [refs.pop(0) for _ in range(n)]
        gate_ref, up_ref = take(2)
        given_refs = take(len(given))
        if final:
            out_refs = take(len(sides))
        else:
            gate_sum, up_sum = take(2)
        arrived, gate_in, up_in = take(3)
        if final:
            gate_sum, up_sum = take(2)
        sem_x, sem_w = take(2)

        def weights_of(i, p):
            part = pl.ds(pl.multiple_of(origins_ref[first + i] * width + p * depth, 128), depth)
            c = i * parts + p
            return (
                pltpu.make_async_copy(gate_ref.at[e, part], gate_in.at[c], sem_w.at[0, c]),
                pltpu.make_async_copy(up_ref.at[e, part], up_in.at[c], sem_w.at[1, c]),
            )

        for i in range(rows):
            for r in range(raw):

                @pl.when(picks_ref[first + i] == base + r)
                def _(r=r, i=i):
                    for p in range(parts):
                        for j in range(number):
                            c = i * parts + p
                            pltpu.make_async_copy(
                                piece_refs[j * raw + r].at[:, pl.ds(p * depth, depth)],
                                arrived.at[c, pl.ds(j * count, count)],
                                sem_x.at[c, j],
                            ).start()

            for p in range(parts):
                for copy in weights_of(i, p):
                    copy.start()
        if given:
            gate_sum[...] = given_refs[0][...]
            up_sum[...] = given_refs[1][...]
        else:
            gate_sum[...] = jnp.zeros_like(gate_sum)
            up_sum[...] = jnp.zeros_like(up_sum)

        for c in range(steps):
            i, p = c // parts, c % parts
            for j in range(number):
                block = pl.ds(j * count, count)
                pltpu.make_async_copy(
                    piece_refs[j * raw].at[:, pl.ds(0, depth)], arrived.at[c, block], sem_x.at[c, j]
                ).wait()
            for copy in weights_of(i, p):
                copy.wait()
            gate_sum[...] += jnp.dot(arrived[c], gate_in[c], preferred_element_type=F32)
            up_sum[...] += jnp.dot(arrived[c], up_in[c], preferred_element_type=F32)

        if not final:
            return
        place = lax.broadcasted_iota(jnp.int32, (CAP, count), 0)
        for j in range(number):
            block = pl.ds(j * count, count)
            value = gate_sum[block]
            hidden = (value / (1.0 + jnp.exp(-value)) * up_sum[block]).astype(BF)
            hot = jnp.where(place == slots_ref[j, e : e + 1, :], 1.0, 0.0).astype(BF)
            ((out_ref, low),) = [(ref, low) for ref, (low, high) in zip(out_refs, sides) if low <= j < high]
            out_ref[pl.ds((j - low) * CAP, CAP), :] = jnp.dot(hot, hidden, preferred_element_type=F32).astype(BF)

    anywhere = pl.BlockSpec(memory_space=pl.ANY)
    scalar = pl.BlockSpec(memory_space=pltpu.SMEM)
    vector = pl.BlockSpec(memory_space=pltpu.VMEM)
    inner = rows * width
    tall = number * count
    held = 2 * (tall * inner + 2 * inner * units) + 20 * tall * units
    sum_shape = jax.ShapeDtypeStruct((tall, units), F32)
    scratch = [
        pltpu.VMEM((steps, tall, depth), BF),
        pltpu.VMEM((steps, depth, units), BF),
        pltpu.VMEM((steps, depth, units), BF),
    ]
    if final:
        scratch += [pltpu.VMEM((tall, units), F32)] * 2
    result = pl.pallas_call(
        body,
        out_shape=[jax.ShapeDtypeStruct(((high - low) * CAP, units), BF) for low, high in sides]
        if final
        else [sum_shape] * 2,
        in_specs=[scalar, scalar, vector] + [anywhere] * (number * raw + 2) + [vector] * len(given),
        out_specs=[vector] * (len(sides) if final else 2),
        scratch_shapes=scratch
        + [pltpu.SemaphoreType.DMA((steps, number)), pltpu.SemaphoreType.DMA((2, steps))],
        compiler_params=pltpu.CompilerParams(
            vmem_limit_bytes=GRANT if held + 8 * 2**20 < GRANT else 63 * 2**20
        ),
        cost_estimate=pl.CostEstimate(
            flops=4 * tall * inner * units,
            bytes_accessed=2 * inner * (tall + 2 * units),
            transcendentals=tall * units,
        ),
        name="gate_up",
    )(picks, origins, slots, *[p for piece in pieces for p in piece], gate_weight, up_weight, *given)
    return result


def down(hidden, picks, origins, down_weight, e, earlier=None, slots=None, weights=None, low=0, cores=1):
    raw = len(hidden)
    rows = picks.shape[0]
    total, units = hidden[0].shape
    inner, width = down_weight.shape[1:]
    tile = tile_of(width, 256)
    chunks = width // tile
    last = earlier is not None
    before = len(earlier) if last else 0
    number, local, count = slots.shape if last else (0, 0, 0)

    def body(picks_ref, origins_ref, *refs):
        refs = list(refs)
        take = lambda n: [refs.pop(0) for _ in range(n)]
        hidden_refs = take(raw)
        (weight_ref,) = take(1)
        earlier_refs = take(before)
        if last:
            slots_ref, weights_ref = take(2)
        out_refs = take(number if last else 1)
        joined, weight_in, sem_h, sem_w = take(4)
        if last:
            held, share, sem_y = take(3)
        for i in range(rows):
            columns = pl.ds(pl.multiple_of(origins_ref[i] * units, 128), units)
            for r in range(raw):

                @pl.when(picks_ref[i] == r)
                def _(r=r):
                    pltpu.make_async_copy(hidden_refs[r], joined.at[:, columns], sem_h.at[i]).start()

        def copy_of(n):
            lanes = pl.ds(pl.multiple_of(n * tile, tile), tile)
            return pltpu.make_async_copy(weight_ref.at[e, :, lanes], weight_in.at[n], sem_w.at[n])

        for n in range(chunks):
            copy_of(n).start()
        if last:
            held_copies = [
                pltpu.make_async_copy(ref.at[pl.ds(low * CAP, total)], held.at[b], sem_y.at[b])
                for b, ref in enumerate(earlier_refs)
            ]
            for copy in held_copies:
                copy.start()
            place = lax.broadcasted_iota(jnp.int32, (CAP, count), 0)
            for j in range(number):
                share[j] = jnp.concatenate(
                    [
                        jnp.where(place == slots_ref[j, b : b + 1, :], weights_ref[j, b : b + 1, :], 0.0)
                        for b in range(local)
                    ],
                    axis=0,
                ).T.astype(BF)
        for i in range(rows):
            columns = pl.ds(pl.multiple_of(origins_ref[i] * units, 128), units)
            pltpu.make_async_copy(hidden_refs[0], joined.at[:, columns], sem_h.at[i]).wait()
        if last:
            for copy in held_copies:
                copy.wait()

        @pl.loop(0, chunks)
        def _(n):
            copy_of(n).wait()
            value = jnp.dot(joined[...], weight_in[n], preferred_element_type=F32).astype(BF)
            lanes = pl.ds(pl.multiple_of(n * tile, tile), tile)
            if not last:
                out_refs[0][:, lanes] = value
                return
            for j in range(number):
                block = slice(j * CAP, (j + 1) * CAP)
                values = jnp.concatenate([held[b, block, lanes] for b in range(before)] + [value[block]], axis=0)
                result = jnp.dot(share[j], values, preferred_element_type=F32)
                out_refs[j][:, lanes] = result.astype(out_refs[j].dtype)

    anywhere = pl.BlockSpec(memory_space=pl.ANY)
    scalar = pl.BlockSpec(memory_space=pltpu.SMEM)
    vector = pl.BlockSpec(memory_space=pltpu.VMEM)
    scratch = [
        pltpu.VMEM((total, inner), BF),
        pltpu.VMEM((chunks, inner, tile), BF),
        pltpu.SemaphoreType.DMA((rows,)),
        pltpu.SemaphoreType.DMA((chunks,)),
    ]
    held_bytes = 2 * (total * inner + inner * width + total * width)
    if last:
        out_shape = [
            jax.ShapeDtypeStruct((count, width), BF if cores == 2 and j % 2 else F32) for j in range(number)
        ]
        scratch += [
            pltpu.VMEM((max(before, 1), total, width), BF),
            pltpu.VMEM((number, count, local * CAP), BF),
            pltpu.SemaphoreType.DMA((max(before, 1),)),
        ]
        held_bytes += 2 * max(before, 1) * total * width + 5 * number * count * width
        extra = [slots, weights]
    else:
        out_shape = [jax.ShapeDtypeStruct((total, width), BF)]
        extra = []
    return pl.pallas_call(
        body,
        out_shape=out_shape,
        in_specs=[scalar, scalar] + [anywhere] * (raw + 1 + before) + [vector] * len(extra),
        out_specs=[vector] * len(out_shape),
        scratch_shapes=scratch,
        compiler_params=pltpu.CompilerParams(vmem_limit_bytes=GRANT if held_bytes + 8 * 2**20 < GRANT else 63 * 2**20),
        cost_estimate=pl.CostEstimate(
            flops=2 * total * inner * width,
            bytes_accessed=2 * (total * inner + inner * width + total * width * (1 + before)),
            transcendentals=0,
        ),
        name="down_combine" if last else "down",
    )(picks, origins, *hidden, down_weight, *(earlier or []), *extra)


def shards(tokens, expert_ids, weight_index, combine_table, gate_weight, up_weight, down_weight):
    links = Links()
    cores, chips = links.cores, links.chips
    local = gate_weight.shape[0]
    experts = local * links.cols
    picks, origins = links.row_tables()
    holds = [has for has, _ in links.row_plan()]

    mine = expert_weights(expert_ids, weight_index, combine_table, experts)
    spread = []
    for distance in range(chips):
        for core in range(cores):
            away = distance or core
            spread.append(links.shift(mine, distance, core) if away else mine)
    spread = jnp.stack(spread)
    weights = lax.dynamic_slice_in_dim(spread, lax.axis_index("col") * local, local, axis=1)
    slots = slots_of(weights)

    held = links.gather_row(tokens, True)
    pieces = []
    for distance in range(chips):
        own = held
        if distance:
            own = [links.shift(v, distance, 0, h) for v, h in zip(held, holds)]
        pieces.append(own)
        if cores == 2:
            pieces.append([links.shift(v, 0, 1, h) for v, h in zip(own, holds)])

    rows = links.rows
    multiply = lambda e, *part, **more: gate_up(pieces, slots, picks, origins, gate_weight, up_weight, e, *part, **more)
    sides = [(0, cores), (cores, links.cols)] if chips > 1 else [(0, cores)]
    early = [multiply(e, 0, rows - 1) for e in range(min(EARLY, local))]
    outs, partial = [], []
    for e in range(local):
        more = {"sides": sides} if e == local - 1 else {}
        if e < len(early):
            hidden = multiply(e, rows - 1, rows, early[e], **more)
        else:
            hidden = multiply(e, 0, rows, **more)
        if e < local - 1:
            hidden = links.gather_row(hidden[0], False)
            outs += down(hidden, picks, origins, down_weight, e)
            continue
        hidden = [links.gather_row(value, False) for value in hidden]
        for side, (low, high) in enumerate(sides):
            partial += down(
                hidden[side], picks, origins, down_weight, e, outs, slots[low:high], weights[low:high], low, cores
            )

    total = None
    for distance in range(chips - 1, -1, -1):
        kept = partial[distance * cores]
        if cores == 2:
            kept = kept + links.shift(partial[distance * cores + 1], 0, 1).astype(F32)
        if distance:
            kept = links.shift(kept.astype(BF), chips - distance, 0).astype(F32)
        total = kept if total is None else total + kept
    return total.astype(BF)


EARLY = 1


def solution(mesh):
    in_specs = (
        P(("grp", "col"), "row"),
        P(("grp", "col"), None),
        P(("grp", "col"), None),
        P(),
        P("col", None, "row"),
        P("col", None, "row"),
        P("col", None, "row"),
    )
    out_specs = P(("grp", "col"), "row")
    return jax.shard_map(shards, mesh=mesh, in_specs=in_specs, out_specs=out_specs, check_vma=False)
```

```python
import jax
import jax.numpy as jnp
from jax import lax
from jax.experimental import pallas as pl
from jax.experimental.pallas import tpu as pltpu
from jax.sharding import PartitionSpec as P

CAP = 80
route_scale = 2.827
BF = jnp.bfloat16
F32 = jnp.float32
GRANT = 44 * 2**20


def tile_of(size, most):
    best = 128
    for width in range(128, most + 1, 128):
        if size % width == 0:
            best = width
    return best if size % best == 0 else size


def combine_weights(weight_index, combine_table):
    table_size = combine_table.shape[0]
    match = weight_index[..., None] == jnp.arange(table_size, dtype=jnp.int32)
    table_values = jnp.sum(jnp.where(match, combine_table, jnp.float32(0.0)), axis=-1)
    return route_scale * table_values / jnp.sum(table_values, axis=-1, keepdims=True)


def expert_weights(expert_ids, weight_index, combine_table, experts):
    weights = combine_weights(weight_index, combine_table)
    match = expert_ids[None] == jnp.arange(experts, dtype=jnp.int32)[:, None, None]
    return jnp.sum(jnp.where(match, weights[None], jnp.float32(0.0)), axis=-1)


def slots_of(weights):
    count = weights.shape[-1]
    named = weights > 0
    row = lax.broadcasted_iota(jnp.int32, (count, count), 0)
    column = lax.broadcasted_iota(jnp.int32, (count, count), 1)
    before = (row < column).astype(BF)
    rank = jnp.einsum("bet,tu->beu", named.astype(BF), before, preferred_element_type=F32)
    return jnp.where(named, rank.astype(jnp.int32), -1)


class Links:
    def __init__(self):
        self.cols = lax.axis_size("col")
        self.rows = lax.axis_size("row")
        self.cores = 2 if self.cols % 2 == 0 else 1
        self.chips = self.cols // self.cores
        self.z = lax.axis_index("row")

    def send(self, value, target, sends=lambda z: True):
        pairs = []
        for col in range(self.cols):
            for z in range(self.rows):
                if sends(z):
                    to_col, to_z = target(col, z)
                    pairs.append((col * self.rows + z, to_col * self.rows + to_z))
        return lax.ppermute(value, ("col", "row"), pairs)

    def shift(self, value, distance, core, holds=lambda z: True):
        step = distance * self.cores
        return self.send(value, lambda col, z: (((col ^ core) + step) % self.cols, z), holds)

    def row_plan(self):
        rows = self.rows
        if rows != 4:
            return [(lambda z, s=s: True, lambda z, s=s: (z - s) % rows) for s in range(rows)]
        return [
            (lambda z: True, lambda z: z),
            (lambda z: z > 0, lambda z: z - 1),
            (lambda z: z < 3, lambda z: z + 1),
            (lambda z: z % 3 == 0, lambda z: 3 - z),
            (lambda z: True, lambda z: (z + 2) % 4),
        ]

    def gather_row(self, value, hops):
        rows = self.rows
        if rows != 4:
            return [value] + [self.send(value, lambda col, z, s=s: (col, (z + s) % rows)) for s in range(1, rows)]
        right = self.send(value, lambda col, z: (col, z + 1), lambda z: z < 3)
        left = self.send(value, lambda col, z: (col, z - 1), lambda z: z > 0)
        if hops:
            end = self.send(value, lambda col, z: (col, 3 - z), lambda z: z in (0, 3))
            right_far = self.send(right, lambda col, z: (col, z + 1), lambda z: z in (1, 2))
            left_far = self.send(left, lambda col, z: (col, z - 1), lambda z: z in (1, 2))
            far = jnp.where(self.z >= 2, right_far, left_far)
        else:
            far = self.send(value, lambda col, z: (col, (z + 2) % 4))
            end = self.send(far, lambda col, z: (col, 3 if z == 2 else 0), lambda z: z in (1, 2))
        return [value, right, left, end, far]

    def row_tables(self):
        plan = self.row_plan()
        picks, origins = [], []
        for z in range(self.rows):
            held = [(r, of(z)) for r, (has, of) in enumerate(plan) if has(z)]
            picks.append([r for r, _ in held])
            origins.append([o for _, o in held])
        take = lambda table: jnp.asarray(table, jnp.int32)[self.z]
        return take(picks), take(origins)


def gate_up(pieces, slots, picks, origins, gate_weight, up_weight, e, first, last, sums=None, sides=None):
    base = len(pieces[0]) - 1 if first else 0
    stop = len(pieces[0]) - (last < picks.shape[0])
    pieces = [piece[base:stop] for piece in pieces]
    number, raw = len(pieces), len(pieces[0])
    every = picks.shape[0]
    rows = last - first
    final = last == every
    count, width = slots.shape[2], gate_weight.shape[1] // every
    _, units = gate_weight.shape[1:]
    given = [] if sums is None else list(sums)
    depth = tile_of(width, 896)
    parts = width // depth
    steps = rows * parts
    sides = sides or [(0, number)]

    def body(picks_ref, origins_ref, slots_ref, *refs):
        piece_refs = refs[: number * raw]
        refs = list(refs[number * raw :])
        take = lambda n: [refs.pop(0) for _ in range(n)]
        gate_ref, up_ref = take(2)
        given_refs = take(len(given))
        if final:
            out_refs = take(len(sides))
        else:
            gate_sum, up_sum = take(2)
        arrived, gate_in, up_in = take(3)
        if final:
            gate_sum, up_sum = take(2)
        sem_x, sem_w = take(2)

        def weights_of(i, p):
            part = pl.ds(pl.multiple_of(origins_ref[first + i] * width + p * depth, 128), depth)
            c = i * parts + p
            return (
                pltpu.make_async_copy(gate_ref.at[e, part], gate_in.at[c], sem_w.at[0, c]),
                pltpu.make_async_copy(up_ref.at[e, part], up_in.at[c], sem_w.at[1, c]),
            )

        for i in range(rows):
            for r in range(raw):

                @pl.when(picks_ref[first + i] == base + r)
                def _(r=r, i=i):
                    for p in range(parts):
                        for j in range(number):
                            c = i * parts + p
                            pltpu.make_async_copy(
                                piece_refs[j * raw + r].at[pl.ds(pieces[j][r][1], count), pl.ds(p * depth, depth)],
                                arrived.at[c, pl.ds(j * count, count)],
                                sem_x.at[c, j],
                            ).start()

            for p in range(parts):
                for copy in weights_of(i, p):
                    copy.start()
        if given:
            gate_sum[...] = given_refs[0][...]
            up_sum[...] = given_refs[1][...]
        else:
            gate_sum[...] = jnp.zeros_like(gate_sum)
            up_sum[...] = jnp.zeros_like(up_sum)

        for c in range(steps):
            i, p = c // parts, c % parts
            for j in range(number):
                block = pl.ds(j * count, count)
                pltpu.make_async_copy(
                    piece_refs[j * raw].at[pl.ds(0, count), pl.ds(0, depth)], arrived.at[c, block], sem_x.at[c, j]
                ).wait()
            for copy in weights_of(i, p):
                copy.wait()
            gate_sum[...] += jnp.dot(arrived[c], gate_in[c], preferred_element_type=F32)
            up_sum[...] += jnp.dot(arrived[c], up_in[c], preferred_element_type=F32)

        if not final:
            return
        place = lax.broadcasted_iota(jnp.int32, (CAP, count), 0)
        for j in range(number):
            block = pl.ds(j * count, count)
            value = gate_sum[block]
            hidden = (value / (1.0 + jnp.exp(-value)) * up_sum[block]).astype(BF)
            hot = jnp.where(place == slots_ref[j, e : e + 1, :], 1.0, 0.0).astype(BF)
            ((out_ref, low),) = [(ref, low) for ref, (low, high) in zip(out_refs, sides) if low <= j < high]
            out_ref[pl.ds((j - low) * CAP, CAP), :] = jnp.dot(hot, hidden, preferred_element_type=F32).astype(BF)

    anywhere = pl.BlockSpec(memory_space=pl.ANY)
    scalar = pl.BlockSpec(memory_space=pltpu.SMEM)
    vector = pl.BlockSpec(memory_space=pltpu.VMEM)
    inner = rows * width
    tall = number * count
    held = 2 * (tall * inner + 2 * inner * units) + 20 * tall * units
    sum_shape = jax.ShapeDtypeStruct((tall, units), F32)
    scratch = [
        pltpu.VMEM((steps, tall, depth), BF),
        pltpu.VMEM((steps, depth, units), BF),
        pltpu.VMEM((steps, depth, units), BF),
    ]
    if final:
        scratch += [pltpu.VMEM((tall, units), F32)] * 2
    result = pl.pallas_call(
        body,
        out_shape=[jax.ShapeDtypeStruct(((high - low) * CAP, units), BF) for low, high in sides]
        if final
        else [sum_shape] * 2,
        in_specs=[scalar, scalar, vector] + [anywhere] * (number * raw + 2) + [vector] * len(given),
        out_specs=[vector] * (len(sides) if final else 2),
        scratch_shapes=scratch
        + [pltpu.SemaphoreType.DMA((steps, number)), pltpu.SemaphoreType.DMA((2, steps))],
        compiler_params=pltpu.CompilerParams(
            vmem_limit_bytes=GRANT if held + 8 * 2**20 < GRANT else 63 * 2**20
        ),
        cost_estimate=pl.CostEstimate(
            flops=4 * tall * inner * units,
            bytes_accessed=2 * inner * (tall + 2 * units),
            transcendentals=tall * units,
        ),
        name="gate_up",
    )(picks, origins, slots, *[p for piece in pieces for p, _ in piece], gate_weight, up_weight, *given)
    return result


def down(hidden, picks, origins, down_weight, e, earlier=None, slots=None, weights=None, low=0, cores=1):
    raw = len(hidden)
    rows = picks.shape[0]
    units = hidden[0].shape[1]
    total = hidden[0].shape[0] if slots is None else slots.shape[0] * CAP
    inner, width = down_weight.shape[1:]
    tile = tile_of(width, 256)
    chunks = width // tile
    last = earlier is not None
    before = len(earlier) if last else 0
    number, local, count = slots.shape if last else (0, 0, 0)

    def body(picks_ref, origins_ref, *refs):
        refs = list(refs)
        take = lambda n: [refs.pop(0) for _ in range(n)]
        hidden_refs = take(raw)
        (weight_ref,) = take(1)
        earlier_refs = take(before)
        if last:
            slots_ref, weights_ref = take(2)
        out_refs = take(number if last else 1)
        joined, weight_in, sem_h, sem_w = take(4)
        if last:
            held, share, sem_y = take(3)
        for i in range(rows):
            columns = pl.ds(pl.multiple_of(origins_ref[i] * units, 128), units)
            for r in range(raw):

                @pl.when(picks_ref[i] == r)
                def _(r=r):
                    pltpu.make_async_copy(
                        hidden_refs[r].at[pl.ds(low * CAP, total)], joined.at[:, columns], sem_h.at[i]
                    ).start()

        def copy_of(n):
            lanes = pl.ds(pl.multiple_of(n * tile, tile), tile)
            return pltpu.make_async_copy(weight_ref.at[e, :, lanes], weight_in.at[n], sem_w.at[n])

        for n in range(chunks):
            copy_of(n).start()
        if last:
            held_copies = [
                pltpu.make_async_copy(ref.at[pl.ds(low * CAP, total)], held.at[b], sem_y.at[b])
                for b, ref in enumerate(earlier_refs)
            ]
            for copy in held_copies:
                copy.start()
            place = lax.broadcasted_iota(jnp.int32, (CAP, count), 0)
            for j in range(number):
                share[j] = jnp.concatenate(
                    [
                        jnp.where(place == slots_ref[j, b : b + 1, :], weights_ref[j, b : b + 1, :], 0.0)
                        for b in range(local)
                    ],
                    axis=0,
                ).T.astype(BF)
        for i in range(rows):
            columns = pl.ds(pl.multiple_of(origins_ref[i] * units, 128), units)
            pltpu.make_async_copy(
                hidden_refs[0].at[pl.ds(low * CAP, total)], joined.at[:, columns], sem_h.at[i]
            ).wait()
        if last:
            for copy in held_copies:
                copy.wait()

        @pl.loop(0, chunks)
        def _(n):
            copy_of(n).wait()
            value = jnp.dot(joined[...], weight_in[n], preferred_element_type=F32).astype(BF)
            lanes = pl.ds(pl.multiple_of(n * tile, tile), tile)
            if not last:
                out_refs[0][:, lanes] = value
                return
            for j in range(number):
                block = slice(j * CAP, (j + 1) * CAP)
                values = jnp.concatenate([held[b, block, lanes] for b in range(before)] + [value[block]], axis=0)
                result = jnp.dot(share[j], values, preferred_element_type=F32)
                out_refs[j][:, lanes] = result.astype(out_refs[j].dtype)

    anywhere = pl.BlockSpec(memory_space=pl.ANY)
    scalar = pl.BlockSpec(memory_space=pltpu.SMEM)
    vector = pl.BlockSpec(memory_space=pltpu.VMEM)
    scratch = [
        pltpu.VMEM((total, inner), BF),
        pltpu.VMEM((chunks, inner, tile), BF),
        pltpu.SemaphoreType.DMA((rows,)),
        pltpu.SemaphoreType.DMA((chunks,)),
    ]
    held_bytes = 2 * (total * inner + inner * width + total * width)
    if last:
        out_shape = [
            jax.ShapeDtypeStruct((count, width), BF if cores == 2 and j % 2 else F32) for j in range(number)
        ]
        scratch += [
            pltpu.VMEM((max(before, 1), total, width), BF),
            pltpu.VMEM((number, count, local * CAP), BF),
            pltpu.SemaphoreType.DMA((max(before, 1),)),
        ]
        held_bytes += 2 * max(before, 1) * total * width + 5 * number * count * width
        extra = [slots, weights]
    else:
        out_shape = [jax.ShapeDtypeStruct((total, width), BF)]
        extra = []
    return pl.pallas_call(
        body,
        out_shape=out_shape,
        in_specs=[scalar, scalar] + [anywhere] * (raw + 1 + before) + [vector] * len(extra),
        out_specs=[vector] * len(out_shape),
        scratch_shapes=scratch,
        compiler_params=pltpu.CompilerParams(vmem_limit_bytes=GRANT if held_bytes + 8 * 2**20 < GRANT else 63 * 2**20),
        cost_estimate=pl.CostEstimate(
            flops=2 * total * inner * width,
            bytes_accessed=2 * (total * inner + inner * width + total * width * (1 + before)),
            transcendentals=0,
        ),
        name="down_combine" if last else "down",
    )(picks, origins, *hidden, down_weight, *(earlier or []), *extra)


def shards(tokens, expert_ids, weight_index, combine_table, gate_weight, up_weight, down_weight):
    links = Links()
    cores, chips = links.cores, links.chips
    local = gate_weight.shape[0]
    experts = local * links.cols
    picks, origins = links.row_tables()
    holds = [has for has, _ in links.row_plan()]

    mine = expert_weights(expert_ids, weight_index, combine_table, experts)
    spread = []
    for distance in range(chips):
        for core in range(cores):
            away = distance or core
            spread.append(links.shift(mine, distance, core) if away else mine)
    spread = jnp.stack(spread)
    weights = lax.dynamic_slice_in_dim(spread, lax.axis_index("col") * local, local, axis=1)
    slots = slots_of(weights)

    held = links.gather_row(tokens, True)
    pieces = []
    for distance in range(chips):
        own = held
        if distance:
            own = [links.shift(v, distance, 0, h) for v, h in zip(held, holds)]
        pieces.append([(v, 0) for v in own])
        if cores == 2:
            joins = [[r] for r in range(len(own))]
            if links.rows == 4:
                joins = [[0], [1], [2], [3], [4]] if distance else [[0], [1, 2], [3], [4]]
            other = []
            for join in joins:
                value = own[join[0]] if len(join) == 1 else jnp.concatenate([own[r] for r in join], axis=0)
                holder = lambda z, join=join: any(holds[r](z) for r in join)
                value = links.shift(value, 0, 1, holder)
                other += [(value, n * own[0].shape[0]) for n in range(len(join))]
            pieces.append(other)

    rows = links.rows
    multiply = lambda e, *part, **more: gate_up(pieces, slots, picks, origins, gate_weight, up_weight, e, *part, **more)
    sides = [(0, cores), (cores, links.cols)] if chips > 1 else [(0, cores)]
    early = [multiply(e, 0, rows - 1) for e in range(min(EARLY, local))]
    outs, partial = [], []
    for e in range(local):
        if e < len(early):
            hidden = multiply(e, rows - 1, rows, early[e])
        else:
            hidden = multiply(e, 0, rows)
        hidden = links.gather_row(hidden[0], False)
        if e < local - 1:
            outs += down(hidden, picks, origins, down_weight, e)
            continue
        for low, high in sides:
            partial += down(
                hidden, picks, origins, down_weight, e, outs, slots[low:high], weights[low:high], low, cores
            )

    total = None
    for distance in range(chips - 1, -1, -1):
        kept = partial[distance * cores]
        if cores == 2:
            kept = kept + links.shift(partial[distance * cores + 1], 0, 1).astype(F32)
        if distance:
            kept = links.shift(kept.astype(BF), chips - distance, 0).astype(F32)
        total = kept if total is None else total + kept
    return total.astype(BF)


EARLY = 1


def solution(mesh):
    in_specs = (
        P(("grp", "col"), "row"),
        P(("grp", "col"), None),
        P(("grp", "col"), None),
        P(),
        P("col", None, "row"),
        P("col", None, "row"),
        P("col", None, "row"),
    )
    out_specs = P(("grp", "col"), "row")
    return jax.shard_map(shards, mesh=mesh, in_specs=in_specs, out_specs=out_specs, check_vma=False)
```
